32 devices in a mesh: pipe: 4 (over z), tp: 2 (over y), dp: 4 (over x, core).
Axes of the slice: x: 2, y: 2, z: 4, core: 2. Of those that a mesh axis runs over, the one named last changes fastest.
Arguments:
- grad_state: bfloat16 [4, 4, 256, 5120], P('pipe', 'dp', 'tp'), may hold values from -6 to 6
- saved_pre: bfloat16 [4, 4, 256, 4096], P('pipe', 'dp', 'tp'), may hold values from -6 to 6
- adapter: bfloat16 [5120, 4096], P('tp', ('pipe', 'dp')), may hold values from -0.09375 to 0.09375
- gain: float32 [4096], replicated, may hold values from 0.5 to 2
Outputs:
- passed_grad: bfloat16 [4, 4, 256, 5120], P('pipe', 'dp', 'tp')
- gain_grad: float32 [4096], replicated
The draws below stay inside these ranges and needn't reach their ends.
All inputs are finite; a program needn't handle non-finite values.
Results may differ from the reference program's by a relative error of at most 0.0054.
Values may be sent and summed in bfloat16 or wider, within the bound.
No kernel may reach another device: no remote copies, remote signals or barrier semaphores. Data moves between devices by JAX's collectives and lax.ppermute only.
A program may use at most 128 MiB of HBM per device.

```python
import math
import jax
import jax.numpy as jnp
from jax import lax

D = 5120
DA = 4096
TOK_SECTION = 256
N_PIPE = 4
N_DP = 4


def with_spikes(values, stream_key, source, target, parts, factor):
    owner, partner = [(jnp.arange(values.shape[position]) // (values.shape[position] // parts)).reshape([-1 if axis == position else 1 for axis in range(values.ndim)]) for position in (source, target)]
    chosen = jax.random.permutation(stream_key, parts)[partner]
    strong = (owner == chosen) | (owner == (partner + parts // 2) % parts)
    return jnp.where(strong, factor * values, values)


def level_of(stream_key, shape, pieces, low, high):
    def one(axis_at, parts):
        draws = jax.random.uniform(jax.random.fold_in(jax.random.fold_in(stream_key, 6), axis_at), (parts,), jnp.float32, low / len(pieces), high / len(pieces))
        return jnp.repeat(jnp.exp(draws), shape[axis_at] // parts).reshape((-1,) + (1,) * (len(shape) - axis_at - 1))

    level = one(*pieces[0])
    for cut in pieces[1:]:
        level = level * one(*cut)
    return level


def gaussian(own_key, extent, spread, reach, split=(), kind=jnp.bfloat16):
    entries = spread * jax.random.normal(own_key, extent, jnp.float32)
    if split:
        entries = entries * level_of(own_key, extent, split, -0.22, 0.18)
    return jnp.clip(entries, -reach, reach).astype(kind)


def noise_with(own_key, dims, width, reach, split, heavy, dtype=jnp.bfloat16):
    array = width * jax.random.normal(own_key, dims, jnp.float32)
    if split:
        array = array * level_of(own_key, dims, split, -0.22, 0.18)
    return jnp.clip(with_spikes(array, jax.random.fold_in(own_key, 3), *heavy), -reach, reach).astype(dtype)


def setup_inputs(seed: int = 0) -> dict:
    keys = jax.random.split(jax.random.key(seed), 5)
    grad_state = noise_with(keys[0], (N_PIPE, N_DP, TOK_SECTION, D), 1.0, 6.0, ((0, 4), (1, 4), (2, 2)), (0, 3, 4, 2.0))
    saved_pre = gaussian(keys[1], (N_PIPE, N_DP, TOK_SECTION, DA), 1.0, 6.0, ((0, 4), (1, 4), (2, 2)))
    adapter = gaussian(keys[2], (D, DA), DA ** -0.5, 0.09375, ((0, 2), (1, 16)))
    gain = jnp.clip(jnp.exp(jax.random.uniform(keys[3], (DA,), jnp.float32, math.log(0.5), math.log(2.0))), 0.5, 2.0)
    return dict(grad_state=grad_state, saved_pre=saved_pre, adapter=adapter, gain=gain)


epsilon = 1e-06

def section_grad(grad_rows, pre_rows, adapter, gain):
    window = grad_rows[:, :DA].astype(jnp.float32)
    pre_vals = pre_rows.astype(jnp.float32)
    inv_rms = lax.rsqrt(lax.optimization_barrier(jnp.mean(pre_vals * pre_vals, axis=-1, keepdims=True)) + epsilon)
    z_hat = pre_vals * inv_rms
    scaled = window * gain
    grad_pre = (inv_rms * (scaled - z_hat * lax.optimization_barrier(jnp.mean(scaled * z_hat, axis=-1, keepdims=True)))).astype(jnp.bfloat16)
    back = lax.dot_general(grad_pre, adapter, (((1,), (1,)), ((), ())), preferred_element_type=jnp.float32).astype(jnp.bfloat16)
    back = lax.optimization_barrier(back)
    result = (grad_rows.astype(jnp.float32) + back.astype(jnp.float32)).astype(jnp.bfloat16)
    return (result, lax.optimization_barrier(jnp.sum(window * z_hat, axis=0)))

def reference(grad_state, saved_pre, adapter, gain):
    groups = N_PIPE * N_DP
    grads = grad_state.reshape(groups, TOK_SECTION, D)
    saved = saved_pre.reshape(groups, TOK_SECTION, DA)
    results, terms = lax.map(lambda pair: section_grad(pair[0], pair[1], adapter, gain), (grads, saved))
    results = results.reshape(N_PIPE, N_DP, TOK_SECTION, D)
    passed_grad = jnp.roll(results, -1, axis=0)
    gain_grad = lax.optimization_barrier(jnp.sum(terms, axis=0)) / jnp.float32(groups)
    return (passed_grad, gain_grad)
```

```python
import functools

import jax
import jax.numpy as jnp
from jax import lax
from jax.experimental import pallas as pl
from jax.experimental.pallas import tpu as pltpu
from jax.sharding import PartitionSpec as P

epsilon = 1e-06


def norm_kernel(half_ref, grad_ref, pre_ref, gain_ref, near_ref, far_ref, terms_ref):
    width = pre_ref.shape[1]
    part = width // 2
    window = grad_ref[...].astype(jnp.float32)
    pre_vals = pre_ref[...].astype(jnp.float32)
    inv_rms = lax.rsqrt(jnp.mean(pre_vals * pre_vals, axis=-1, keepdims=True) + epsilon)
    z_hat = pre_vals * inv_rms
    scaled = window * gain_ref[...]
    grad_pre = (
        inv_rms * (scaled - z_hat * jnp.mean(scaled * z_hat, axis=-1, keepdims=True))
    ).astype(jnp.bfloat16)

    @pl.when(half_ref[0] == 0)
    def _():
        near_ref[...] = grad_pre[:, :part]
        far_ref[...] = grad_pre[:, part:]

    @pl.when(half_ref[0] != 0)
    def _():
        near_ref[...] = grad_pre[:, part:]
        far_ref[...] = grad_pre[:, :part]

    @pl.when(pl.program_id(0) == 0)
    def _():
        terms_ref[...] = jnp.zeros_like(terms_ref)

    terms_ref[...] += jnp.sum(window * z_hat, axis=0, keepdims=True)


def norm_backward(half, grad_rows, pre_rows, gain):
    rows, width = pre_rows.shape
    block = 32 if rows % 32 == 0 else rows
    part = width // 2
    return pl.pallas_call(
        norm_kernel,
        grid_spec=pltpu.PrefetchScalarGridSpec(
            num_scalar_prefetch=1,
            grid=(rows // block,),
            in_specs=[
                pl.BlockSpec((block, width), lambda i, s: (i, 0)),
                pl.BlockSpec((block, width), lambda i, s: (i, 0)),
                pl.BlockSpec((1, width), lambda i, s: (0, 0)),
            ],
            out_specs=[
                pl.BlockSpec((block, part), lambda i, s: (i, 0)),
                pl.BlockSpec((block, part), lambda i, s: (i, 0)),
                pl.BlockSpec((1, width), lambda i, s: (0, 0)),
            ],
        ),
        out_shape=[
            jax.ShapeDtypeStruct((rows, part), jnp.bfloat16),
            jax.ShapeDtypeStruct((rows, part), jnp.bfloat16),
            jax.ShapeDtypeStruct((1, width), jnp.float32),
        ],
        cost_estimate=pl.CostEstimate(
            flops=20 * rows * width, bytes_accessed=6 * rows * width, transcendentals=rows
        ),
        name="norm_backward",
    )(half[None], grad_rows, pre_rows, gain[None])


def product_kernel(splits, count, with_grad, at_ref, *refs):
    rows_refs = refs[:splits]
    piece_refs = refs[splits : splits + count]
    grad_refs = refs[splits + count : -1]
    out_ref = refs[-1]
    depth = piece_refs[0].shape[1]
    total = None
    for index, piece in enumerate(piece_refs):
        columns = pl.ds(pl.multiple_of(at_ref[index] * depth, depth), depth)
        left = jnp.concatenate([ref[:, columns] for ref in rows_refs], axis=0)
        term = lax.dot_general(
            left, piece[...], (((1,), (1,)), ((), ())), preferred_element_type=jnp.float32
        )
        total = term if total is None else total + term
    rows = rows_refs[0].shape[0]
    for index in range(splits):
        block = total[index * rows : (index + 1) * rows]
        if with_grad:
            block = block + grad_refs[index][...].astype(jnp.float32)
        out_ref[index] = block.astype(out_ref.dtype)


def partial_product(at, blocks, pieces, grads, name):
    splits, count = len(blocks), len(pieces)
    rows, part = blocks[0].shape
    columns, depth = pieces[0].shape
    if depth % 128:
        left = jnp.concatenate(blocks, axis=0)
        total = jnp.zeros((splits * rows, columns), jnp.float32)
        for index, piece in enumerate(pieces):
            own = lax.dynamic_slice_in_dim(left, at[index] * depth, depth, 1)
            total = total + lax.dot_general(
                own, piece, (((1,), (1,)), ((), ())), preferred_element_type=jnp.float32
            )
        total = total.reshape(splits, rows, columns)
        if grads:
            total = total + jnp.stack(grads).astype(jnp.float32)
        return total.astype(jnp.bfloat16)
    tile = 256 if columns % 256 == 0 else columns
    return pl.pallas_call(
        functools.partial(product_kernel, splits, count, bool(grads)),
        grid_spec=pltpu.PrefetchScalarGridSpec(
            num_scalar_prefetch=1,
            grid=(columns // tile,),
            in_specs=[pl.BlockSpec((rows, part), lambda i, s: (0, 0))] * splits
            + [pl.BlockSpec((tile, depth), lambda i, s: (i, 0))] * count
            + [pl.BlockSpec((rows, tile), lambda i, s: (0, i))] * len(grads),
            out_specs=pl.BlockSpec((splits, rows, tile), lambda i, s: (0, 0, i)),
        ),
        out_shape=jax.ShapeDtypeStruct((splits, rows, columns), jnp.bfloat16),
        cost_estimate=pl.CostEstimate(
            flops=2 * splits * rows * columns * depth * count,
            bytes_accessed=2
            * (splits * rows * part + count * columns * depth + 2 * splits * rows * columns),
            transcendentals=0,
        ),
        name=name,
    )(at, *blocks, *pieces, *grads)


def rotated(value, axis, steps):
    count = lax.axis_size(axis)
    if steps % count == 0:
        return value
    return lax.ppermute(value, axis, [(i, (i + steps) % count) for i in range(count)])


def crossed(value, axis, bits):
    return lax.ppermute(value, axis, [(i, i ^ bits) for i in range(lax.axis_size(axis))])


def per_device(grad_state, saved_pre, adapter, gain):
    grad_rows = grad_state[0, 0]
    pre_rows = saved_pre[0, 0]
    planes, splits, replicas = (lax.axis_size(a) for a in ("pipe", "tp", "dp"))
    group = planes // 2
    plane, split, replica = (lax.axis_index(a) for a in ("pipe", "tp", "dp"))
    half, place = plane // group, plane % group
    wide = grad_rows.shape[1] // splits
    chunks = 2 if wide % 512 == 0 else 1
    chunk = wide // chunks

    def across(value):
        pairs = []
        for s in range(planes):
            h, p = s // group, s % group
            pairs.append((s, (1 - h) * group + (p - 1) % group))
        return lax.ppermute(value, "pipe", pairs)

    def in_group(value, steps):
        if steps % group == 0:
            return value
        pairs = []
        for s in range(planes):
            h, p = s // group, s % group
            pairs.append((s, h * group + (p - steps) % group))
        return lax.ppermute(value, "pipe", pairs)

    def from_split(value, steps):
        return rotated(value, "tp", -steps)

    at = jnp.stack(
        [
            ((place + steps) % group) * replicas + (replica ^ far ^ near)
            for near in (0, 1)
            for far in range(0, replicas, 2)
            for steps in range(group)
        ]
    ).astype(jnp.int32)

    pieces = []
    for c in range(chunks):
        own = lax.slice_in_dim(adapter, c * chunk, (c + 1) * chunk, axis=0)
        local = [in_group(own, steps) for steps in range(group)]
        same = []
        for far in range(0, replicas, 2):
            same += [v if far == 0 else crossed(v, "dp", far) for v in local]
        pieces.append(same + [crossed(v, "dp", 1) for v in same])

    grads = []
    for steps in range(splits):
        block = lax.dynamic_slice_in_dim(
            grad_rows, ((split - steps) % splits) * wide, wide, 1
        )
        grads.append(from_split(block, steps))

    near_part, far_part, terms = norm_backward(half, grad_rows, pre_rows, gain)
    moved = across(far_part)
    near_blocks = [from_split(near_part, steps) for steps in range(splits)]
    far_blocks = [from_split(moved, steps) for steps in range(splits)]

    total = terms
    for axis in ("dp", "tp", "pipe"):
        bit = 1
        while bit < lax.axis_size(axis):
            total = total + crossed(total, axis, bit)
            bit *= 2
    gain_grad = (total / jnp.float32(planes * replicas))[0]

    last = place == group - 1
    swap_pairs = []
    for s in range(planes):
        if s % group != group - 1:
            swap_pairs.append((s, (s + group) % planes))
    finals = []
    for c in range(chunks):
        cut = [lax.slice_in_dim(g, c * chunk, (c + 1) * chunk, axis=1) for g in grads]
        native = partial_product(at, near_blocks, pieces[c], cut, "native_product")
        other = partial_product(at, far_blocks, pieces[c], [], "other_product")
        native = rotated(native, "pipe", -1)
        arrived = lax.ppermute(other, "pipe", swap_pairs)
        rest = jnp.where(last, other, arrived)
        final = (native.astype(jnp.float32) + rest.astype(jnp.float32)).astype(jnp.bfloat16)
        finals.append([rotated(final[steps], "tp", steps) for steps in range(splits)])

    columns = []
    for q in range(splits):
        which = (split - q) % splits
        for c in range(chunks):
            if splits == 2:
                columns.append(jnp.where(which == 0, finals[c][0], finals[c][1]))
            else:
                columns.append(lax.select_n(which, *finals[c]))
    passed = jnp.concatenate(columns, axis=1)
    return (passed[None, None], gain_grad)


def solution(mesh):
    placed = (
        P("pipe", "dp", "tp", None),
        P("pipe", "dp", "tp", None),
        P("tp", ("pipe", "dp")),
        P(),
    )
    return jax.shard_map(
        per_device,
        mesh=mesh,
        in_specs=placed,
        out_specs=(P("pipe", "dp", "tp", None), P()),
        check_vma=False,
    )
```
